128 devices in a mesh: section: 8 (over x, core), seq: 16 (over z, y).
Axes of the slice: x: 4, y: 4, z: 4, core: 2. Of those that a mesh axis runs over, the one named last changes fastest.
Arguments:
- residual: bfloat16 [8, 4096, 2048], P('section', 'seq'), may hold values from -6 to 6
- w_qkv: bfloat16 [8, 2048, 6144], P('section', 'seq'), may hold values from -0.125 to 0.125
- w_beta: bfloat16 [8, 2048, 16], P('section', 'seq'), may hold values from -0.125 to 0.125
- beta_bias: float32 [8, 16], P('section'), may hold values from -8 to 2
- norm_gain: float32 [8, 2048], P('section'), may hold values from 0.1 to 1.9
- out_gain: float32 [8, 128], P('section'), may hold values from 0.1 to 1.9
- state_in: float32 [8, 16, 128, 128], P('section'), may hold values from -6 to 6
- doc_start: int32 [2, 8], P(None, 'section'), may hold values from 0 to 64, as said below
Outputs:
- stream_out: bfloat16 [8, 4096, 2048], P('section', 'seq')
The draws below stay inside these ranges and needn't reach their ends.
Inputs may be any that keep to these rules, and one draw needn't show every extreme that they name: `doc_start`: 64 means no new document in that micro-batch.
All inputs are finite; a program needn't handle non-finite values.
Results may differ from the reference program's by a relative error of at most 0.03.
Values may be sent and summed in bfloat16 or wider, within the bound.
No kernel may reach another device: no remote copies, remote signals or barrier semaphores. Data moves between devices by JAX's collectives and lax.ppermute only.
A program may use at most 192 MiB of HBM per device.

```python
import jax
import jax.numpy as jnp
from jax import lax

HEADS = 16
HD = 128
D = 2048
GROUP = 64
TICKS = 2
LAYERS = 8
SEQ = 4096
NCH = 64


def draw_beta_bias(key, part):
    return jax.random.uniform(key, (LAYERS, HEADS), jnp.float32, -7.0, 2.0)


def draw_doc_start(key, part):
    drawn = jax.random.randint(key, (TICKS, LAYERS), 0, NCH + 1, dtype=jnp.int32)
    drawn = drawn.at[0, 0].set(NCH)
    return drawn.at[1, 0].set(0)


def levels(rng, extent, split, low, high):
    level, own = 1.0, jax.random.fold_in(rng, 6)
    for dim, blocks in split:
        draws = jnp.exp(jax.random.uniform(jax.random.fold_in(own, dim), (blocks,), jnp.float32, low / len(split), high / len(split)))
        level = level * jnp.repeat(draws, extent[dim] // blocks).reshape([-1 if axis == dim else 1 for axis in range(len(extent))])
    return level


def scatter_about(rng, extent, deviation, most, cuts=(), kind=jnp.bfloat16):
    entries = deviation * jax.random.normal(rng, extent, jnp.float32)
    if cuts:
        entries = entries * levels(rng, extent, cuts, -0.22, 0.18)
    return jnp.clip(entries, -most, most).astype(kind)


def setup_inputs(seed: int = 0) -> dict:
    key_of = jax.random.split(jax.random.key(seed), 9)
    return {
        "residual": scatter_about(key_of[0], (LAYERS, SEQ, D), 1.0, 6.0, ((0, 8), (1, 16))),
        "w_qkv": scatter_about(key_of[1], (LAYERS, D, 3 * D), D ** -0.5, 0.125, ((0, 8), (1, 16))),
        "w_beta": scatter_about(key_of[2], (LAYERS, D, HEADS), D ** -0.5, 0.125, ((0, 8), (1, 16))),
        "beta_bias": draw_beta_bias(jax.random.fold_in(key_of[8], 71), 0),
        "norm_gain": jnp.clip(1.0 + 0.18 * jax.random.normal(key_of[4], (LAYERS, D), jnp.float32), 0.1, 1.9),
        "out_gain": jnp.clip(1.0 + 0.18 * jax.random.normal(key_of[5], (LAYERS, HD), jnp.float32), 0.1, 1.9),
        "state_in": scatter_about(key_of[6], (LAYERS, HEADS, HD, HD), 1.0, 6.0, ((0, 8),), jnp.float32),
        "doc_start": draw_doc_start(jax.random.fold_in(key_of[8], 71), 0),
    }


FULL_PRECISION = lax.Precision.HIGHEST

def unit_norm(projected):
    return projected * lax.rsqrt(lax.optimization_barrier(jnp.sum(projected * projected, axis=-1, keepdims=True)) + 1e-06)

def block_solve(key_rows, values, beta_rows):
    block_len = key_rows.shape[-2]
    intersections = jnp.einsum('ghik,ghjk->ghij', key_rows, key_rows, precision=FULL_PRECISION)
    system = jnp.tril(intersections * beta_rows[..., :, None], -1) + jnp.eye(block_len, dtype=jnp.float32)
    right_side = jnp.concatenate([values * beta_rows[..., None], key_rows * beta_rows[..., None]], axis=-1)
    solved = lax.linalg.triangular_solve(system, right_side, left_side=True, lower=True, unit_diagonal=True)
    head_width = values.shape[-1]
    return (solved[..., :head_width], solved[..., head_width:])

def prepare(stream, weight_qkv, weight_beta, head_bias, in_gain):
    row_count = stream.shape[0]
    widened = stream.astype(jnp.float32)
    normed = (widened * lax.rsqrt(lax.optimization_barrier(jnp.mean(widened * widened, axis=-1, keepdims=True)) + 1e-05) * in_gain).astype(jnp.bfloat16)
    projected = jnp.dot(normed.astype(jnp.float32), weight_qkv.astype(jnp.float32), preferred_element_type=jnp.float32).reshape(row_count, 3, HEADS, HD)
    queries = unit_norm(projected[:, 0]).astype(jnp.bfloat16)
    key_rows = unit_norm(projected[:, 1]).astype(jnp.bfloat16)
    values = projected[:, 2].astype(jnp.bfloat16)
    beta_rows = jax.nn.sigmoid(jnp.dot(normed.astype(jnp.float32), weight_beta.astype(jnp.float32), preferred_element_type=jnp.float32) + head_bias)
    blocks = row_count // GROUP

    def to_blocks(tensor):
        return tensor.astype(jnp.float32).reshape(blocks, GROUP, HEADS, HD).transpose(0, 2, 1, 3)
    beta_blk = beta_rows.reshape(blocks, GROUP, HEADS).transpose(0, 2, 1)
    key_block = to_blocks(key_rows)
    inject, weights = block_solve(key_block, to_blocks(values), beta_blk)
    return (to_blocks(queries), key_block, inject, weights, widened)

def run_blocks(queries, key_rows, inject, weights, current_state, doc_block, first_block):
    block_count = queries.shape[0]
    block_len = queries.shape[2]
    causal = jnp.tril(jnp.ones((block_len, block_len), jnp.float32))

    def advance(current_state, pieces):
        query_block, key_block, inject_block, weight_block, block_index = pieces
        current_state = jnp.where(block_index == doc_block, jnp.zeros_like(current_state), current_state)
        delta_values = inject_block - jnp.einsum('jxy,jyu->jxu', weight_block, current_state, precision=FULL_PRECISION)
        attention_scores = jnp.einsum('hik,hjk->hij', query_block, key_block, precision=FULL_PRECISION) * causal
        block_result = jnp.einsum('jxy,jyu->jxu', query_block, current_state, precision=FULL_PRECISION) + jnp.einsum('ucd,udo->uco', attention_scores, delta_values, precision=FULL_PRECISION)
        current_state = current_state + jnp.einsum('plq,plw->pqw', key_block, delta_values, precision=FULL_PRECISION)
        return (current_state, block_result)
    block_ids = first_block + jnp.arange(block_count, dtype=jnp.int32)
    return lax.scan(advance, current_state, (queries, key_rows, inject, weights, block_ids))

def finish(widened, block_result, head_gain):
    blocks = block_result.shape[0]
    mixed = block_result.transpose(0, 2, 1, 3).reshape(blocks * GROUP, HEADS, HD)
    mixed = mixed * lax.rsqrt(lax.optimization_barrier(jnp.mean(mixed * mixed, axis=-1, keepdims=True)) + 1e-05) * head_gain
    return (widened + mixed.reshape(blocks * GROUP, HEADS * HD)).astype(jnp.bfloat16)

def reference(residual, w_qkv, w_beta, beta_bias, norm_gain, out_gain, state_in, doc_start):

    def segment_pass(pieces):
        stream, weight_qkv, weight_beta, head_bias, in_gain, head_gain, given_state, doc_block = pieces
        queries, key_rows, inject, weights, widened = prepare(stream, weight_qkv, weight_beta, head_bias, in_gain)
        final_state, block_result = run_blocks(queries, key_rows, inject, weights, given_state, doc_block, jnp.int32(0))
        return (finish(widened, block_result, head_gain), final_state)
    stream = residual
    carried = state_in
    outputs = residual
    for tick_index in range(TICKS):
        outputs, carried = lax.map(segment_pass, (stream, w_qkv, w_beta, beta_bias, norm_gain, out_gain, carried, doc_start[tick_index]))
        stream = jnp.roll(outputs, 1, axis=0)
    return outputs
```

```python
import functools

import jax
import jax.numpy as jnp
from jax import lax
from jax.experimental import pallas as pl
from jax.experimental.pallas import tpu as pltpu
from jax.sharding import Mesh, PartitionSpec as P

HEADS = 16
HD = 128
D = 2048
GROUP = 64
TICKS = 2
SIDE = 4
OWN = HEADS // SIDE
ROWS = 1024
CH = 128
GROUPS = ((0, 1), (2, 3))
BF = jnp.bfloat16
F32 = jnp.float32


def dot(a, b):
    return jnp.dot(a, b, preferred_element_type=F32)


def dot_nt(a, b):
    return lax.dot_general(a, b, (((1,), (1,)), ((), ())), preferred_element_type=F32)


def dot_tn(a, b):
    return lax.dot_general(a, b, (((0,), (0,)), ((), ())), preferred_element_type=F32)


def shift(value, axis, by, count=SIDE):
    return lax.ppermute(value, axis, [(i, (i + by) % count) for i in range(count)])


def around(value, axis):
    half = value.shape[0] // 2
    left = shift(value, axis, 1)
    right = shift(value, axis, -1)
    top = shift(left[:half], axis, 1)
    bottom = shift(right[half:], axis, -1)
    return value, left, right, top, bottom


STEPS = (0, -1, 1, 2)


def call(kernel, name, outs, ins, args, scratch=(), flops=0, vmem=48 << 20):
    nbytes = sum(a.size * a.dtype.itemsize for a in args)
    return pl.pallas_call(
        kernel,
        out_shape=outs,
        in_specs=ins,
        out_specs=jax.tree.map(lambda _: pl.BlockSpec(memory_space=pltpu.VMEM), outs),
        scratch_shapes=list(scratch),
        name=name,
        compiler_params=pltpu.CompilerParams(vmem_limit_bytes=vmem),
        cost_estimate=pl.CostEstimate(flops=flops, bytes_accessed=nbytes, transcendentals=0),
    )(*args)


SM = pl.BlockSpec(memory_space=pltpu.SMEM)
VM = pl.BlockSpec(memory_space=pltpu.VMEM)


def feature_block(where, p, s):
    z = lax.rem(where[0] + STEPS[p] + SIDE, SIDE)
    y = lax.rem(where[1] - s + SIDE, SIDE)
    return z * SIDE + y


def write_normed(where, read, scale, gain_ref, normed_ref, rows):
    for p in range(SIDE):
        for s in range(SIDE):
            at = pl.multiple_of(feature_block(where, p, s) * HD, HD)
            part = read(at).astype(F32) * scale * gain_ref[:, pl.ds(at, HD)]
            normed_ref[rows, (p * SIDE + s) * HD : (p * SIDE + s + 1) * HD] = part.astype(BF)


def write_beta(normed_ref, wb_ref, bias_ref, beta_ref, rows):
    logits = dot_nt(normed_ref[rows, :], wb_ref[...]) + bias_ref[...]
    beta_ref[rows, :] = 1.0 / (1.0 + jnp.exp(-logits))


def norm_rows_kernel(where, own, left, right, top, bottom, gain_ref, wb_ref, bias_ref, normed_ref, beta_ref, res_ref):
    tile = 128
    for ref, step, off, size in ((own, 0, 0, 256), (left, -1, 0, 256), (right, 1, 0, 256), (top, 2, 0, 128), (bottom, 2, 128, 128)):
        base = lax.rem(where[1] + step + SIDE, SIDE) * 256 + off

        def block(i, carry, ref=ref, base=base):
            src = pl.ds(pl.multiple_of(i * tile, tile), tile)
            rows = pl.ds(pl.multiple_of(base + i * tile, tile), tile)
            x = ref[src, :].astype(F32)
            scale = lax.rsqrt(jnp.mean(x * x, axis=-1, keepdims=True) + 1e-05)
            write_normed(where, lambda at: ref[src, pl.ds(at, HD)], scale, gain_ref, normed_ref, rows)
            res_ref[rows, :] = ref[src, pl.ds(pl.multiple_of(where[1] * 512, 512), 512)]
            write_beta(normed_ref, wb_ref, bias_ref, beta_ref, rows)
            return carry

        lax.fori_loop(0, size // tile, block, 0)


def norm_columns_kernel(where, *refs):
    sets = [refs[5 * g : 5 * g + 5] for g in range(len(GROUPS))]
    gain_ref, wb_ref, bias_ref, normed_ref, beta_ref, x_ref = refs[5 * len(GROUPS) :]
    tile = 128
    for g, pieces in enumerate(sets):
        width = len(GROUPS[g]) * HD
        for ref, step, off in zip(pieces, (0, -1, 1, 2, 2), (0, 0, 0, 0, ROWS // 2)):
            at = lax.rem(where[1] + step + SIDE, SIDE) * 512 + GROUPS[g][0] * HD
            x_ref[off : off + ref.shape[0], pl.ds(pl.multiple_of(at, HD), width)] = ref[...]

    def block(i, carry):
        rows = pl.ds(pl.multiple_of(i * tile, tile), tile)
        x = x_ref[rows, :].astype(F32)
        scale = lax.rsqrt(jnp.mean(x * x, axis=-1, keepdims=True) + 1e-05)
        write_normed(where, lambda at: x_ref[rows, pl.ds(at, HD)], scale, gain_ref, normed_ref, rows)
        write_beta(normed_ref, wb_ref, bias_ref, beta_ref, rows)
        return carry

    lax.fori_loop(0, ROWS // tile, block, 0)


def local_kernel(heads, where, normed_ref, beta_ref, *refs):
    w_refs = refs[:5]
    p_ref, m_ref, qkv_ref, state_ref, mask_ref = refs[5:]
    nh = len(heads)
    width = nh * HD

    offsets = (0, 512, 1024, 1536, 1792)
    sizes = (512, 512, 512, 256, 256)
    for part in range(3):
        cols = slice(part * width, (part + 1) * width)

        def project(i, carry, part=part, cols=cols):
            rows = pl.ds(pl.multiple_of(i * 512, 512), 512)
            acc = None
            for w_ref, off, size in zip(w_refs, offsets, sizes):
                term = dot(normed_ref[rows, off : off + size], w_ref[:, cols])
                acc = term if acc is None else acc + term
            for h in range(nh):
                one = acc[:, h * HD : (h + 1) * HD]
                if part < 2:
                    one = one * lax.rsqrt(jnp.sum(one * one, axis=-1, keepdims=True) + 1e-06)
                qkv_ref[rows, (part * nh + h) * HD : (part * nh + h + 1) * HD] = one.astype(BF)
            return carry

        lax.fori_loop(0, ROWS // 512, project, 0)

    row = lax.broadcasted_iota(jnp.int32, (CH, CH), 0)
    col = lax.broadcasted_iota(jnp.int32, (CH, CH), 1)
    for level in range(7):
        rb, cb = lax.shift_right_logical(row, level), lax.shift_right_logical(col, level)
        inside = (lax.rem(rb, 2) == 1) & (cb == rb - 1)
        mask_ref[level] = jnp.where(inside, 1.0, 0.0).astype(BF)
    eye = jnp.where(row == col, 1.0, 0.0)
    wide_col = lax.broadcasted_iota(jnp.int32, (CH, 2 * HD), 1)
    wide_row = lax.broadcasted_iota(jnp.int32, (CH, 2 * HD), 0)
    for h in range(nh):
        state_ref[h] = jnp.where(wide_col == wide_row, 1.0, 0.0)

    per = 2

    def chunks(i, carry):
        doc = where[2]
        items = [(c, h) for c in range(per) for h in range(nh)]
        base = [pl.multiple_of((i * per + c) * CH, CH) for c in range(per)]
        near = [doc - base[c] for c in range(per)]
        apart = [(col < near[c]) & (near[c] <= row) for c in range(per)]
        entry = [jnp.where((near[c] >= 0) & (near[c] <= row), 0.0, 1.0).astype(BF) for c in range(per)]
        leave = [jnp.where((row < near[c]) & (near[c] <= CH - 1), 0.0, 1.0).astype(BF) for c in range(per)]
        keep = [jnp.where((near[c] >= 0) & (near[c] <= CH - 1), 0.0, 1.0) for c in range(per)]
        rows = [pl.ds(base[c], CH) for c in range(per)]

        def part(c, h, which):
            return qkv_ref[rows[c], (which * nh + h) * HD : (which * nh + h + 1) * HD]

        q = [part(c, h, 0) for c, h in items]
        k = [part(c, h, 1) for c, h in items]
        v = [part(c, h, 2) for c, h in items]
        b = [jnp.broadcast_to(beta_ref[rows[c], heads[h] : heads[h] + 1], (CH, HD)) for c, h in items]
        n = range(len(items))
        both = [dot_nt(jnp.concatenate([q[t], k[t]], axis=0), k[t]) for t in n]
        attn, low = [], []
        for t, (c, h) in enumerate(items):
            attn.append(jnp.where((row >= col) & ~apart[c], both[t][:CH], 0.0).astype(BF))
            low.append(jnp.where((row > col) & ~apart[c], both[t][CH:] * b[t], 0.0).astype(BF))
        inv = [eye - (low[t] * mask_ref[0]).astype(F32) for t in n]
        for level in range(1, 7):
            short = [inv[t].astype(BF) for t in n]
            mid = [dot(low[t] * mask_ref[level], short[t]).astype(BF) for t in n]
            inv = [inv[t] - dot(short[t], mid[t]) for t in n]
        right = []
        for t, (c, h) in enumerate(items):
            bk = (k[t].astype(F32) * b[t]).astype(BF) * entry[c]
            right.append(jnp.concatenate([bk, (v[t].astype(F32) * b[t]).astype(BF)], axis=1))
        wu = [dot(inv[t].astype(BF), right[t]) for t in n]
        weight = [wu[t][:, :HD].astype(BF) for t in n]
        inject = [jnp.concatenate([jnp.zeros((CH, HD), F32), wu[t][:, HD:]], axis=1) for t in n]
        left = [jnp.concatenate([q[t] * entry[c], attn[t]], axis=1) for t, (c, h) in enumerate(items)]
        kept = [k[t] * leave[c] for t, (c, h) in enumerate(items)]
        for t, (c, h) in enumerate(items):
            state = state_ref[h]
            short = state.astype(BF)
            delta = (inject[t] - dot(weight[t], short)).astype(BF)
            state_ref[h] = state * keep[c] + dot_tn(kept[t], delta)
            result = dot(left[t], jnp.concatenate([short, delta], axis=0))
            p_ref[rows[c], h * 2 * HD : (h + 1) * 2 * HD] = result.astype(BF)
        return carry

    lax.fori_loop(0, ROWS // CH // per, chunks, 0)
    for h in range(nh):
        m_ref[h] = state_ref[h].astype(BF)


def finish_kernel(nh, offset, where, m0, m1, m2, m3, s_ref, p_ref, x_ref, gain_ref, out_ref, final_ref, maps_ref):
    for s, ref in enumerate((m0, m1, m2, m3)):
        maps_ref[lax.rem(where[0] - s + SIDE, SIDE)] = ref[...]
    entries = []
    states = [s_ref[h] for h in range(nh)]
    firsts = list(states)
    for z in range(SIDE):
        for h in range(nh):
            firsts[h] = jnp.where(where[0] == z, states[h], firsts[h])
        for h in range(nh):
            high = states[h].astype(BF)
            low = (states[h] - high.astype(F32)).astype(BF)
            a = maps_ref[z, h, :, :HD]
            states[h] = dot(a, high) + dot(a, low) + maps_ref[z, h, :, HD:].astype(F32)
    for h in range(nh):
        final_ref[h] = states[h]
        entries.append(firsts[h].astype(BF))

    def block(i, carry):
        rows = pl.ds(pl.multiple_of(i * 256, 256), 256)
        for h in range(nh):
            pa = p_ref[rows, h * 2 * HD : h * 2 * HD + HD]
            pb = p_ref[rows, h * 2 * HD + HD : (h + 1) * 2 * HD]
            o = dot(pa, entries[h]) + pb.astype(F32)
            o = o * lax.rsqrt(jnp.mean(o * o, axis=-1, keepdims=True) + 1e-05) * gain_ref[...]
            x = x_ref[rows, offset + h * HD : offset + (h + 1) * HD].astype(F32)
            out_ref[rows, h * HD : (h + 1) * HD] = (x + o).astype(BF)
        return carry

    lax.fori_loop(0, ROWS // 256, block, 0)


def place_kernel(where, *refs):
    out_ref = refs[-1]
    for g in range(len(GROUPS)):
        for s in range(SIDE):
            ref = refs[g * SIDE + s]
            at = lax.rem(where[1] - s + SIDE, SIDE) * 512 + GROUPS[g][0] * HD
            out_ref[:, pl.ds(pl.multiple_of(at, HD), ref.shape[1])] = ref[...]


def struct(shape, dtype=BF):
    return jax.ShapeDtypeStruct(shape, dtype)


def shards(residual, w_qkv, w_beta, beta_bias, norm_gain, out_gain, state_in, doc_start):
    z, y = lax.axis_index("z"), lax.axis_index("y")
    w5 = w_qkv[0].reshape(HD, 3, SIDE, OWN, HD)

    weights = []
    for heads in GROUPS:
        parts = []
        for s in range(SIDE):
            mine = lax.dynamic_index_in_dim(w5, (y + s) % SIDE, axis=2, keepdims=False)
            mine = mine[:, :, heads[0] : heads[-1] + 1, :].reshape(HD, 3 * len(heads) * HD)
            parts.append(shift(mine, "y", s) if s else mine)
        weights.append(around(jnp.concatenate(parts, axis=0), "z"))
    x_pieces = around(residual[0], "y")
    wb = w_beta[0].T
    wb = jnp.concatenate([wb] + [shift(wb, "y", s) for s in range(1, SIDE)], axis=1)
    wb = jnp.concatenate([wb] + [shift(wb, "z", -s) for s in STEPS[1:]], axis=1)
    wb = jnp.pad(lax.dynamic_slice_in_dim(wb, y * OWN, OWN, axis=0), ((0, HD - OWN), (0, 0)))
    bias = jnp.pad(lax.dynamic_slice_in_dim(beta_bias[0], y * OWN, OWN), (0, HD - OWN))[None]
    given = lax.dynamic_slice_in_dim(state_in[0], y * OWN, OWN, axis=0)
    states = [given[heads[0] : heads[-1] + 1] for heads in GROUPS]

    for tick in range(TICKS):
        where = jnp.stack([z, y, doc_start[tick, 0] * GROUP - z * ROWS]).astype(jnp.int32)
        norm_outs = [struct((ROWS, D)), struct((ROWS, HD), F32)]
        tail = (norm_gain, wb, bias)
        if tick == 0:
            normed, beta, res = call(
                norm_rows_kernel, "norm_rows", norm_outs + [struct((ROWS, OWN * HD))], [SM] + [VM] * 8, (where, *x_pieces, *tail)
            )
            residuals = [(res, heads[0] * HD) for heads in GROUPS]
        else:
            flat = [piece for pieces in columns for piece in pieces]
            normed, beta = call(
                norm_columns_kernel,
                "norm_columns",
                norm_outs,
                [SM] + [VM] * (len(flat) + 3),
                (where, *flat, *tail),
                scratch=[pltpu.VMEM((ROWS, D), BF)],
            )
            residuals = [(pieces[0], 0) for pieces in columns]
        columns, finals = [], []
        for g, heads in enumerate(GROUPS):
            nh = len(heads)
            p, m = call(
                functools.partial(local_kernel, heads),
                "local",
                [struct((ROWS, nh * 2 * HD)), struct((nh, HD, 2 * HD))],
                [SM] + [VM] * 7,
                (where, normed, beta, *weights[g]),
                scratch=[
                    pltpu.VMEM((ROWS, 3 * nh * HD), BF),
                    pltpu.VMEM((nh, HD, 2 * HD), F32),
                    pltpu.VMEM((7, CH, CH), BF),
                ],
                flops=nh * 6 * ROWS * D * HD,
            )
            maps = [m] + [shift(m, "z", s) for s in range(1, SIDE)]
            res, offset = residuals[g]
            out, states[g] = call(
                functools.partial(finish_kernel, nh, offset),
                "finish",
                [struct((ROWS, nh * HD)), struct((nh, HD, HD), F32)],
                [SM] + [VM] * 8,
                (where, *maps, states[g], p, res, out_gain),
                scratch=[pltpu.VMEM((SIDE, nh, HD, 2 * HD), BF)],
            )
            if tick + 1 < TICKS:
                columns.append(around(shift(out, "section", 1, lax.axis_size("section")), "y"))
            else:
                for s in range(SIDE):
                    rows = lax.dynamic_slice_in_dim(out, (y + s) % SIDE * 256, 256, axis=0)
                    finals.append(shift(rows, "y", s) if s else rows)
    out = call(place_kernel, "place", [struct((256, D))], [SM] + [VM] * len(finals), (where, *finals))[0]
    return out[None]


def solution(mesh):
    split = Mesh(mesh.devices.reshape(mesh.devices.shape[0], SIDE, SIDE), ("section", "z", "y"))
    wide = P("section", ("z", "y"), None)
    return jax.shard_map(
        shards,
        mesh=split,
        in_specs=(
            wide,
            wide,
            wide,
            P("section", None),
            P("section", None),
            P("section", None),
            P("section", None, None, None),
            P(None, "section"),
        ),
        out_specs=wide,
        check_vma=False,
    )
```

```python
import functools

import jax
import jax.numpy as jnp
from jax import lax
from jax.experimental import pallas as pl
from jax.experimental.pallas import tpu as pltpu
from jax.sharding import Mesh, PartitionSpec as P

HEADS = 16
HD = 128
D = 2048
GROUP = 64
TICKS = 2
SIDE = 4
OWN = HEADS // SIDE
ROWS = 1024
CH = 128
BASE = 8
LEVELS = (8, 16, 32, 64)
PER = 4
GROUPS = ((0, 1), (2, 3))
BF = jnp.bfloat16
F32 = jnp.float32


def dot(a, b):
    return jnp.dot(a, b, preferred_element_type=F32)


def dot_nt(a, b):
    return lax.dot_general(a, b, (((1,), (1,)), ((), ())), preferred_element_type=F32)


def dot_tn(a, b):
    return lax.dot_general(a, b, (((0,), (0,)), ((), ())), preferred_element_type=F32)


def shift(value, axis, by, count=SIDE):
    return lax.ppermute(value, axis, [(i, (i + by) % count) for i in range(count)])


def around(value, axis, forward):
    left = shift(value, axis, 1)
    right = shift(value, axis, -1)
    across = shift(left, axis, 1) if forward else shift(right, axis, -1)
    return value, left, right, across


def after(value, *others):
    return lax.optimization_barrier((value, *others))[0]


STEPS = (0, -1, 1, 2)


def call(kernel, name, outs, ins, args, scratch=(), flops=0, vmem=16 << 20, grid=()):
    nbytes = sum(a.size * a.dtype.itemsize for a in args)
    return pl.pallas_call(
        kernel,
        out_shape=outs,
        in_specs=ins,
        out_specs=jax.tree.map(lambda _: pl.BlockSpec(memory_space=pltpu.VMEM), outs),
        scratch_shapes=list(scratch),
        grid=grid,
        name=name,
        compiler_params=pltpu.CompilerParams(vmem_limit_bytes=vmem),
        cost_estimate=pl.CostEstimate(flops=flops, bytes_accessed=nbytes, transcendentals=0),
    )(*args)


SM = pl.BlockSpec(memory_space=pltpu.SMEM)
VM = pl.BlockSpec(memory_space=pltpu.VMEM)
HBM = pl.BlockSpec(memory_space=pltpu.HBM)


def feature_block(where, p, s):
    z = lax.rem(where[0] + STEPS[p] + SIDE, SIDE)
    y = lax.rem(where[1] - s + SIDE, SIDE)
    return z * SIDE + y


def write_normed(where, read, scale, gain_ref, normed_ref, rows):
    for p in range(SIDE):
        for s in range(SIDE):
            at = pl.multiple_of(feature_block(where, p, s) * HD, HD)
            part = read(at).astype(F32) * scale * gain_ref[:, pl.ds(at, HD)]
            normed_ref[rows, (p * SIDE + s) * HD : (p * SIDE + s + 1) * HD] = part.astype(BF)


TILE = 128


def layer_kernel(tick, where, bias_ref, *refs):
    count = 1 if tick == 0 else SIDE * len(GROUPS)
    sources, refs = refs[:count], refs[count:]
    gain_ref, refs = refs[0], refs[1:]
    w_sources, refs = refs[: 5 * len(GROUPS)], refs[5 * len(GROUPS) :]
    p_ref, m_ref = refs[:2]
    res_ref, refs = (refs[2], refs[3:]) if tick == 0 else (None, refs[2:])
    x_ref, w0_ref, w1_ref, normed_ref, beta_ref, qkv_ref, state_ref, mask_ref, x_sems, w_sems = refs
    arrivals = []
    for at, ref in enumerate(sources):
        step = STEPS[at % SIDE]
        base = lax.rem(where[1] + step + SIDE, SIDE)
        if tick == 0:
            target = x_ref
        else:
            heads = GROUPS[at // SIDE]
            base = pl.multiple_of(base * (OWN * HD) + heads[0] * HD, HD)
            target = x_ref.at[:, pl.ds(base, len(heads) * HD)]
        arrivals.append(pltpu.make_async_copy(ref, target, x_sems.at[at]))
        arrivals[-1].start()
    w_arrivals = []
    for at, ref in enumerate(w_sources):
        start = (0, 512, 1024, 1536, 1792)[at % 5]
        target = (w0_ref, w1_ref)[at // 5].at[start : start + ref.shape[0]]
        w_arrivals.append(pltpu.make_async_copy(ref, target, w_sems.at[at]))
        w_arrivals[-1].start()

    for copy in arrivals:
        copy.wait()

    def normalize(i, carry):
        rows = pl.ds(pl.multiple_of(i * TILE, TILE), TILE)
        x = x_ref[rows, :].astype(F32)
        scale = lax.rsqrt(jnp.mean(x * x, axis=-1, keepdims=True) + 1e-05)
        write_normed(where, lambda at: x_ref[rows, pl.ds(at, HD)], scale, gain_ref, normed_ref, rows)
        if tick == 0:
            res_ref[rows, :] = x_ref[rows, pl.ds(pl.multiple_of(where[1] * 512, 512), 512)]
        return carry

    lax.fori_loop(0, ROWS // TILE, normalize, 0)
    for copy in w_arrivals:
        copy.wait()
    lane = lax.broadcasted_iota(jnp.int32, (1, HD), 1)
    bias = jnp.zeros((1, HD), F32)
    for h in range(OWN):
        bias = jnp.where(lane == h, bias_ref[0, where[1] * OWN + h], bias)
    logits = dot(normed_ref[...], w0_ref[:, 3 * len(GROUPS[0]) * HD :]) + bias
    beta_ref[...] = 1.0 / (1.0 + jnp.exp(-logits))

    width = len(GROUPS[0]) * HD
    for g in range(len(GROUPS)):
        def project(part, carry, g=g):
            cols = pl.ds(pl.multiple_of(part * width, width), width)
            acc = dot(normed_ref[...], (w0_ref, w1_ref)[g][:, cols])
            for h in range(width // HD):
                one = acc[:, h * HD : (h + 1) * HD]
                scale = lax.rsqrt(jnp.sum(one * one, axis=-1, keepdims=True) + 1e-06)
                scale = jnp.where(part < 2, scale, 1.0)
                qkv_ref[g, :, pl.ds(pl.multiple_of(part * width + h * HD, HD), HD)] = (one * scale).astype(BF)
            return carry

        lax.fori_loop(0, 3, project, 0)

    heads = range(OWN)
    nh = OWN
    row = lax.broadcasted_iota(jnp.int32, (CH, CH), 0)
    col = lax.broadcasted_iota(jnp.int32, (CH, CH), 1)
    lane = lax.broadcasted_iota(jnp.int32, (BASE, CH), 1)
    place = lax.broadcasted_iota(jnp.int32, (BASE, CH), 0)
    diagonal = (row // BASE) == (col // BASE)
    mask_ref[0] = jnp.where(diagonal, 1.0, 0.0)
    for level, size in enumerate(LEVELS):
        inside = (row // size) == (col // size) + 1
        mask_ref[level + 1] = jnp.where(inside, 1.0, 0.0)
    spread = jnp.where(diagonal, 1.0, 0.0).astype(BF)
    wide_col = lax.broadcasted_iota(jnp.int32, (CH, 2 * HD), 1)
    wide_row = lax.broadcasted_iota(jnp.int32, (CH, 2 * HD), 0)
    for h in range(nh):
        state_ref[h] = jnp.where(wide_col == wide_row, 1.0, 0.0)

    per = PER

    def chunks(i, carry):
        doc = where[2]
        items = [(c, h) for c in range(per) for h in range(nh)]
        base = [pl.multiple_of((i * per + c) * CH, CH) for c in range(per)]
        near = [doc - base[c] for c in range(per)]
        apart = [(col < near[c]) & (near[c] <= row) for c in range(per)]
        entry = [jnp.where((near[c] >= 0) & (near[c] <= row), 0.0, 1.0).astype(BF) for c in range(per)]
        leave = [jnp.where((row < near[c]) & (near[c] <= CH - 1), 0.0, 1.0).astype(BF) for c in range(per)]
        keep = [jnp.where((near[c] >= 0) & (near[c] <= CH - 1), 0.0, 1.0) for c in range(per)]
        rows = [pl.ds(base[c], CH) for c in range(per)]

        def part(c, h, which):
            at = (which * 2 + h % 2) * HD
            return qkv_ref[h // 2, rows[c], at : at + HD]

        q = [part(c, h, 0) for c, h in items]
        k = [part(c, h, 1) for c, h in items]
        v = [part(c, h, 2) for c, h in items]
        b = [jnp.broadcast_to(beta_ref[rows[c], heads[h] : heads[h] + 1], (CH, HD)) for c, h in items]
        n = range(len(items))
        both = [dot_nt(jnp.concatenate([q[t], k[t]], axis=0), k[t]) for t in n]
        attn, low = [], []
        for t, (c, h) in enumerate(items):
            attn.append(jnp.where((row >= col) & ~apart[c], both[t][:CH], 0.0).astype(BF))
            low.append(jnp.where((row > col) & ~apart[c], both[t][CH:] * b[t], 0.0))
        small = []
        for t in n:
            on = low[t] * mask_ref[0]
            small.append(sum(on[r * BASE : (r + 1) * BASE] for r in range(CH // BASE)))
        picked = [jnp.concatenate([jnp.where((lane & (BASE - 1)) == j, small[t], 0.0) for j in range(BASE)], axis=0) for t in n]
        factors = [dot(picked[t].astype(BF), spread) for t in n]
        tops = [jnp.where((lane & (BASE - 1)) == place, 1.0, 0.0) for t in n]
        for j in range(BASE - 1):
            tops = [tops[t] - factors[t][j * BASE : (j + 1) * BASE] * tops[t][j : j + 1] for t in n]
        inv = [jnp.concatenate([tops[t]] * (CH // BASE), axis=0) * mask_ref[0] for t in n]
        for level, size in enumerate(LEVELS):
            blocks = range(CH // size)

            def odd(value):
                return jnp.concatenate([value[r * size : (r + 1) * size] for r in blocks if r % 2], axis=0)

            def mixed(even, odds):
                pieces = []
                for r in blocks:
                    at = r // 2 * size
                    pieces.append(odds[at : at + size] if r % 2 else even(r))
                return jnp.concatenate(pieces, axis=0)

            below = [(odd(low[t]) * odd(mask_ref[level + 1])).astype(BF) for t in n]
            mid = [dot(below[t], inv[t].astype(BF)) for t in n]
            mid = [mixed(lambda r: jnp.zeros((size, CH), F32), mid[t]).astype(BF) for t in n]
            rest = [odd(inv[t]) for t in n]
            rest = [rest[t] - dot(rest[t].astype(BF), mid[t]) for t in n]
            inv = [mixed(lambda r: inv[t][r * size : (r + 1) * size], rest[t]) for t in n]
        right = []
        for t, (c, h) in enumerate(items):
            bk = (k[t].astype(F32) * b[t]).astype(BF) * entry[c]
            right.append(jnp.concatenate([bk, (v[t].astype(F32) * b[t]).astype(BF)], axis=1))
        wu = [dot(inv[t].astype(BF), right[t]) for t in n]
        weight = [wu[t][:, :HD].astype(BF) for t in n]
        inject = [jnp.concatenate([jnp.zeros((CH, HD), F32), wu[t][:, HD:]], axis=1) for t in n]
        left = [jnp.concatenate([q[t] * entry[c], attn[t]], axis=1) for t, (c, h) in enumerate(items)]
        kept = [k[t] * leave[c] for t, (c, h) in enumerate(items)]
        for t, (c, h) in enumerate(items):
            state = state_ref[h]
            short = state.astype(BF)
            delta = (inject[t] - dot(weight[t], short)).astype(BF)
            state_ref[h] = state * keep[c] + dot_tn(kept[t], delta)
            result = dot(left[t], jnp.concatenate([short, delta], axis=0))
            p_ref[rows[c], h * 2 * HD : (h + 1) * 2 * HD] = result.astype(BF)
        return carry

    lax.fori_loop(0, ROWS // CH // per, chunks, 0)
    for h in range(nh):
        m_ref[h] = state_ref[h].astype(BF)


def finish_kernel(nh, split, where, m0, m1, m2, m3, s_ref, p_ref, x_refs, gain_ref, out_refs, final_ref, maps_ref):
    for s, ref in enumerate((m0, m1, m2, m3)):
        maps_ref[lax.rem(where[0] - s + SIDE, SIDE)] = ref[...]
    states = [s_ref[h] for h in range(nh)]
    firsts = list(states)
    for z in range(SIDE):
        for h in range(nh):
            firsts[h] = jnp.where(where[0] == z, states[h], firsts[h])
        if split and z == SIDE - 1:
            break
        for h in range(nh):
            high = states[h].astype(BF)
            low = (states[h] - high.astype(F32)).astype(BF)
            a = maps_ref[z, h, :, :HD]
            states[h] = dot(a, high) + dot(a, low) + maps_ref[z, h, :, HD:].astype(F32)
    if not split:
        for h in range(nh):
            final_ref[h] = states[h]
    entries = [first.astype(BF) for first in firsts]

    def finish(rows, outs, out_rows):
        for h in range(nh):
            pa = p_ref[rows, h * 2 * HD : h * 2 * HD + HD]
            pb = p_ref[rows, h * 2 * HD + HD : (h + 1) * 2 * HD]
            o = dot(pa, entries[h]) + pb.astype(F32)
            o = o * lax.rsqrt(jnp.mean(o * o, axis=-1, keepdims=True) + 1e-05) * gain_ref[...]
            x_ref = x_refs[h * len(x_refs) // nh]
            at = h % (nh // len(x_refs)) * HD
            x = x_ref[rows, at : at + HD].astype(F32)
            at = h % (nh // len(outs)) * HD
            outs[h * len(outs) // nh][out_rows, at : at + HD] = (x + o).astype(BF)

    if split:
        for s in range(SIDE):
            rows = pl.ds(pl.multiple_of(lax.rem(where[1] + s, SIDE) * 256, 256), 256)
            finish(rows, out_refs[s : s + 1], slice(None))
    else:

        def block(i, carry):
            rows = pl.ds(pl.multiple_of(i * 256, 256), 256)
            finish(rows, out_refs, rows)
            return carry

        lax.fori_loop(0, ROWS // 256, block, 0)


def finish_first_kernel(nh, *refs):
    finish_kernel(nh, False, *refs[:7], (refs[7],), *refs[8:9], refs[9:11], *refs[11:])


def finish_last_kernel(nh, *refs):
    finish_kernel(nh, True, *refs[:7], refs[7:9], refs[9], refs[10:14], None, refs[14])


def pack_kernel(where, w_ref, wb_ref, *out_refs):
    for g, heads in enumerate(GROUPS):
        width = len(heads) * HD
        for s in range(SIDE):
            for part in range(3):
                at = part * D + lax.rem(where[1] + s, SIDE) * (OWN * HD) + heads[0] * HD
                columns = w_ref[:, pl.ds(pl.multiple_of(at, HD), width)]
                out_refs[g * SIDE + s][:, part * width : (part + 1) * width] = columns
    source = lax.broadcasted_iota(jnp.int32, (HEADS, HD), 0)
    target = lax.broadcasted_iota(jnp.int32, (HEADS, HD), 1)
    for s in range(SIDE):
        chosen = (source == target + lax.rem(where[1] + s, SIDE) * OWN) & (target < OWN)
        out_refs[s][:, 3 * len(GROUPS[0]) * HD :] = dot(wb_ref[...], jnp.where(chosen, 1.0, 0.0).astype(BF)).astype(BF)


def join_kernel(*refs):
    for s in range(SIDE):
        refs[-1][s * HD : (s + 1) * HD] = refs[s][...]


def place_kernel(where, *refs):
    for s in range(SIDE):
        at = lax.rem(where[1] - s + SIDE, SIDE) * (OWN * HD)
        refs[-1][:, pl.ds(pl.multiple_of(at, OWN * HD), OWN * HD)] = refs[s][...]


def struct(shape, dtype=BF):
    return jax.ShapeDtypeStruct(shape, dtype)


def shards(residual, w_qkv, w_beta, beta_bias, norm_gain, out_gain, state_in, doc_start):
    z, y = lax.axis_index("z"), lax.axis_index("y")
    here = jnp.stack([z, y]).astype(jnp.int32)

    width = 3 * len(GROUPS[0]) * HD
    widths = (width + HD, width)
    packs = [struct((HD, wide)) for wide in widths for _ in range(SIDE)]
    packed = call(pack_kernel, "pack", packs, [SM, VM, VM], (here, w_qkv[0], w_beta[0]))
    sent = []
    for g in range(len(GROUPS)):
        mine = packed[g * SIDE : g * SIDE + SIDE]
        if sent:
            mine = after(tuple(mine), *sent[-1][1:])
        sent.append([mine[0]] + [shift(mine[s], "y", s) for s in range(1, SIDE)])
    weights = []
    for g in range(len(GROUPS)):
        joined = call(join_kernel, "join", [struct((SIDE * HD, widths[g]))], [VM] * SIDE, tuple(sent[g]))[0]
        left, right = shift(joined, "z", 1), shift(joined, "z", -1)
        half = joined.shape[0] // 2
        weights.append((joined, left, right, shift(left[:half], "z", 1), shift(right[half:], "z", -1)))
    flat = [piece for pieces in weights for piece in pieces]
    x = after(residual[0], *sent[0][1:])
    pieces = [lax.all_gather(x, "y", axis=0, tiled=True)]
    states = lax.dynamic_slice_in_dim(state_in[0], y * OWN, OWN, axis=0)

    for tick in range(TICKS):
        where = jnp.stack([z, y, doc_start[tick, 0] * GROUP - z * ROWS]).astype(jnp.int32)
        outs = [struct((ROWS, OWN * 2 * HD)), struct((OWN, HD, 2 * HD))]
        scratch = [
            pltpu.VMEM((ROWS, D), BF),
            pltpu.VMEM((D, widths[0]), BF),
            pltpu.VMEM((D, widths[1]), BF),
            pltpu.VMEM((ROWS, D), BF),
            pltpu.VMEM((ROWS, HD), F32),
            pltpu.VMEM((len(GROUPS), ROWS, width), BF),
            pltpu.VMEM((OWN, HD, 2 * HD), F32),
            pltpu.VMEM((1 + len(LEVELS), CH, CH), F32),
            pltpu.SemaphoreType.DMA((len(pieces),)),
            pltpu.SemaphoreType.DMA((len(flat),)),
        ]
        if tick == 0:
            outs.append(struct((ROWS, OWN * HD)))
        p, m, *rest = call(
            functools.partial(layer_kernel, tick),
            "layer",
            outs,
            [SM, SM] + [HBM] * len(pieces) + [VM] + [HBM] * len(flat),
            (where, beta_bias, *pieces, norm_gain, *flat),
            scratch=scratch,
            flops=8 * ROWS * D * OWN * HD,
            vmem=60 << 20,
        )
        maps = [m] + [shift(m, "z", s) for s in range(1, SIDE)]
        if tick + 1 < TICKS:
            pieces = []
            *outs, states = call(
                functools.partial(finish_first_kernel, OWN),
                "finish",
                [struct((ROWS, OWN * HD // len(GROUPS)))] * len(GROUPS) + [struct((OWN, HD, HD), F32)],
                [SM] + [VM] * 8,
                (where, *maps, states, p, rest[0], out_gain),
                scratch=[pltpu.VMEM((SIDE, OWN, HD, 2 * HD), BF)],
            )
            moved = [shift(out, "section", 1, lax.axis_size("section")) for out in outs]
            for g in range(len(GROUPS)):
                pieces.extend(around(moved[g], "y", g == 0))
        else:
            outs = call(
                functools.partial(finish_last_kernel, OWN),
                "finish_last",
                [struct((256, OWN * HD))] * SIDE,
                [SM] + [VM] * 9,
                (where, *maps, states, p, pieces[0], pieces[SIDE], out_gain),
                scratch=[pltpu.VMEM((SIDE, OWN, HD, 2 * HD), BF)],
            )
    outs = [outs[0]] + [shift(outs[s], "y", s) for s in range(1, SIDE)]
    out = call(place_kernel, "place", [struct((256, D))], [SM] + [VM] * SIDE, (here, *outs))[0]
    return out[None]


def solution(mesh):
    split = Mesh(mesh.devices.reshape(mesh.devices.shape[0], SIDE, SIDE), ("section", "z", "y"))
    wide = P("section", ("z", "y"), None)
    return jax.shard_map(
        shards,
        mesh=split,
        in_specs=(
            wide,
            wide,
            wide,
            P("section", None),
            P("section", None),
            P("section", None),
            P("section", None, None, None),
            P(None, "section"),
        ),
        out_specs=wide,
        check_vma=False,
    )
```

```python
import functools

import jax
import jax.numpy as jnp
from jax import lax
from jax.experimental import pallas as pl
from jax.experimental.pallas import tpu as pltpu
from jax.sharding import Mesh, PartitionSpec as P

HEADS = 16
HD = 128
D = 2048
GROUP = 64
TICKS = 2
SIDE = 4
OWN = HEADS // SIDE
ROWS = 1024
CH = 128
BASE = 8
LEVELS = (8, 16, 32, 64)
PER = 4
GROUPS = ((0, 1), (2, 3))
BF = jnp.bfloat16
F32 = jnp.float32


def dot(a, b):
    return jnp.dot(a, b, preferred_element_type=F32)


def dot_nt(a, b):
    return lax.dot_general(a, b, (((1,), (1,)), ((), ())), preferred_element_type=F32)


def dot_tn(a, b):
    return lax.dot_general(a, b, (((0,), (0,)), ((), ())), preferred_element_type=F32)


def shift(value, axis, by, count=SIDE):
    return lax.ppermute(value, axis, [(i, (i + by) % count) for i in range(count)])


def around(value, axis, forward):
    left = shift(value, axis, 1)
    right = shift(value, axis, -1)
    across = shift(left, axis, 1) if forward else shift(right, axis, -1)
    return value, left, right, across


def halves_around(value, axis, *others):
    left, right = shift(value, axis, 1), shift(value, axis, -1)
    half = value.shape[0] // 2
    passed = after((left, right), *others) if others else (left, right)
    return value, left, right, shift(passed[0][:half], axis, 1), shift(passed[1][half:], axis, -1)


def after(value, *others):
    return lax.optimization_barrier((value, *others))[0]


STEPS = (0, -1, 1, 2)


def call(kernel, name, outs, ins, args, scratch=(), flops=0, vmem=16 << 20, grid=()):
    nbytes = sum(a.size * a.dtype.itemsize for a in args)
    return pl.pallas_call(
        kernel,
        out_shape=outs,
        in_specs=ins,
        out_specs=jax.tree.map(lambda _: pl.BlockSpec(memory_space=pltpu.VMEM), outs),
        scratch_shapes=list(scratch),
        grid=grid,
        name=name,
        compiler_params=pltpu.CompilerParams(vmem_limit_bytes=vmem),
        cost_estimate=pl.CostEstimate(flops=flops, bytes_accessed=nbytes, transcendentals=0),
    )(*args)


SM = pl.BlockSpec(memory_space=pltpu.SMEM)
VM = pl.BlockSpec(memory_space=pltpu.VMEM)
HBM = pl.BlockSpec(memory_space=pltpu.HBM)


def feature_block(where, p, s):
    z = lax.rem(where[0] + STEPS[p] + SIDE, SIDE)
    y = lax.rem(where[1] - s + SIDE, SIDE)
    return z * SIDE + y


def write_normed(where, read, scale, gain_ref, normed_ref, rows):
    for p in range(SIDE):
        for s in range(SIDE):
            at = pl.multiple_of(feature_block(where, p, s) * HD, HD)
            part = read(at).astype(F32) * scale * gain_ref[:, pl.ds(at, HD)]
            normed_ref[rows, (p * SIDE + s) * HD : (p * SIDE + s + 1) * HD] = part.astype(BF)


TILE = 128


def layer_kernel(tick, where, bias_ref, *refs):
    count = 5 if tick == 0 else SIDE * len(GROUPS)
    sources, refs = refs[:count], refs[count:]
    gain_ref, refs = refs[0], refs[1:]
    w_sources, refs = refs[: 5 * len(GROUPS)], refs[5 * len(GROUPS) :]
    p_ref, m_ref = refs[:2]
    res_ref, refs = (refs[2], refs[3:]) if tick == 0 else (None, refs[2:])
    x_ref, w0_ref, w1_ref, normed_ref, beta_ref, qkv_ref, state_ref, mask_ref, x_sems, w_sems = refs
    arrivals = []
    for at, ref in enumerate(sources):
        step = (STEPS + STEPS[-1:])[at] if tick == 0 else STEPS[at % SIDE]
        base = lax.rem(where[1] + step + SIDE, SIDE)
        if tick == 0:
            size = ref.shape[0]
            target = x_ref.at[pl.ds(pl.multiple_of(base * 256 + (size if at == 4 else 0), size), size)]
        else:
            heads = GROUPS[at // SIDE]
            base = pl.multiple_of(base * (OWN * HD) + heads[0] * HD, HD)
            target = x_ref.at[:, pl.ds(base, len(heads) * HD)]
        arrivals.append(pltpu.make_async_copy(ref, target, x_sems.at[at]))
        arrivals[-1].start()
    for copy in arrivals:
        copy.wait()
    w_arrivals = []
    for at, ref in enumerate(w_sources):
        start = (0, 512, 1024, 1536, 1792)[at % 5]
        target = (w0_ref, w1_ref)[at // 5].at[start : start + ref.shape[0]]
        w_arrivals.append(pltpu.make_async_copy(ref, target, w_sems.at[at]))
        w_arrivals[-1].start()

    def normalize(i, carry):
        rows = pl.ds(pl.multiple_of(i * TILE, TILE), TILE)
        x = x_ref[rows, :].astype(F32)
        scale = lax.rsqrt(jnp.mean(x * x, axis=-1, keepdims=True) + 1e-05)
        write_normed(where, lambda at: x_ref[rows, pl.ds(at, HD)], scale, gain_ref, normed_ref, rows)
        if tick == 0:
            res_ref[rows, :] = x_ref[rows, pl.ds(pl.multiple_of(where[1] * 512, 512), 512)]
        return carry

    lax.fori_loop(0, ROWS // TILE, normalize, 0)
    for copy in w_arrivals:
        copy.wait()
    lane = lax.broadcasted_iota(jnp.int32, (1, HD), 1)
    bias = jnp.zeros((1, HD), F32)
    for h in range(OWN):
        bias = jnp.where(lane == h, bias_ref[0, where[1] * OWN + h], bias)
    logits = dot(normed_ref[...], w0_ref[:, 3 * len(GROUPS[0]) * HD :]) + bias
    beta_ref[...] = 1.0 / (1.0 + jnp.exp(-logits))

    width = len(GROUPS[0]) * HD
    for g in range(len(GROUPS)):
        def project(part, carry, g=g):
            cols = pl.ds(pl.multiple_of(part * width, width), width)
            acc = dot(normed_ref[...], (w0_ref, w1_ref)[g][:, cols])
            for h in range(width // HD):
                one = acc[:, h * HD : (h + 1) * HD]
                scale = lax.rsqrt(jnp.sum(one * one, axis=-1, keepdims=True) + 1e-06)
                scale = jnp.where(part < 2, scale, 1.0)
                qkv_ref[g, :, pl.ds(pl.multiple_of(part * width + h * HD, HD), HD)] = (one * scale).astype(BF)
            return carry

        lax.fori_loop(0, 3, project, 0)

    heads = range(OWN)
    nh = OWN
    row = lax.broadcasted_iota(jnp.int32, (CH, CH), 0)
    col = lax.broadcasted_iota(jnp.int32, (CH, CH), 1)
    lane = lax.broadcasted_iota(jnp.int32, (BASE, CH), 1)
    place = lax.broadcasted_iota(jnp.int32, (BASE, CH), 0)
    diagonal = (row // BASE) == (col // BASE)
    mask_ref[0] = jnp.where(diagonal, 1.0, 0.0)
    for level, size in enumerate(LEVELS):
        inside = (row // size) == (col // size) + 1
        mask_ref[level + 1] = jnp.where(inside, 1.0, 0.0)
    spread = jnp.where(diagonal, 1.0, 0.0).astype(BF)
    wide_col = lax.broadcasted_iota(jnp.int32, (CH, 2 * HD), 1)
    wide_row = lax.broadcasted_iota(jnp.int32, (CH, 2 * HD), 0)
    for h in range(nh):
        state_ref[h] = jnp.where(wide_col == wide_row, 1.0, 0.0)

    per = PER

    def chunks(i, carry):
        doc = where[2]
        items = [(c, h) for c in range(per) for h in range(nh)]
        base = [pl.multiple_of((i * per + c) * CH, CH) for c in range(per)]
        near = [doc - base[c] for c in range(per)]
        apart = [(col < near[c]) & (near[c] <= row) for c in range(per)]
        entry = [jnp.where((near[c] >= 0) & (near[c] <= row), 0.0, 1.0).astype(BF) for c in range(per)]
        leave = [jnp.where((row < near[c]) & (near[c] <= CH - 1), 0.0, 1.0).astype(BF) for c in range(per)]
        keep = [jnp.where((near[c] >= 0) & (near[c] <= CH - 1), 0.0, 1.0) for c in range(per)]
        rows = [pl.ds(base[c], CH) for c in range(per)]

        def part(c, h, which):
            at = (which * 2 + h % 2) * HD
            return qkv_ref[h // 2, rows[c], at : at + HD]

        q = [part(c, h, 0) for c, h in items]
        k = [part(c, h, 1) for c, h in items]
        v = [part(c, h, 2) for c, h in items]
        b = [jnp.broadcast_to(beta_ref[rows[c], heads[h] : heads[h] + 1], (CH, HD)) for c, h in items]
        n = range(len(items))
        both = [dot_nt(jnp.concatenate([q[t], k[t]], axis=0), k[t]) for t in n]
        attn, low = [], []
        for t, (c, h) in enumerate(items):
            attn.append(jnp.where((row >= col) & ~apart[c], both[t][:CH], 0.0).astype(BF))
            low.append(jnp.where((row > col) & ~apart[c], both[t][CH:] * b[t], 0.0))
        small = []
        for t in n:
            on = low[t] * mask_ref[0]
            small.append(sum(on[r * BASE : (r + 1) * BASE] for r in range(CH // BASE)))
        picked = [jnp.concatenate([jnp.where((lane & (BASE - 1)) == j, small[t], 0.0) for j in range(BASE)], axis=0) for t in n]
        factors = [dot(picked[t].astype(BF), spread) for t in n]
        tops = [jnp.where((lane & (BASE - 1)) == place, 1.0, 0.0) for t in n]
        for j in range(BASE - 1):
            tops = [tops[t] - factors[t][j * BASE : (j + 1) * BASE] * tops[t][j : j + 1] for t in n]
        inv = [jnp.concatenate([tops[t]] * (CH // BASE), axis=0) * mask_ref[0] for t in n]
        for level, size in enumerate(LEVELS):
            blocks = range(CH // size)

            def odd(value):
                return jnp.concatenate([value[r * size : (r + 1) * size] for r in blocks if r % 2], axis=0)

            def mixed(even, odds):
                pieces = []
                for r in blocks:
                    at = r // 2 * size
                    pieces.append(odds[at : at + size] if r % 2 else even(r))
                return jnp.concatenate(pieces, axis=0)

            below = [(odd(low[t]) * odd(mask_ref[level + 1])).astype(BF) for t in n]
            mid = [dot(below[t], inv[t].astype(BF)) for t in n]
            mid = [mixed(lambda r: jnp.zeros((size, CH), F32), mid[t]).astype(BF) for t in n]
            rest = [odd(inv[t]) for t in n]
            rest = [rest[t] - dot(rest[t].astype(BF), mid[t]) for t in n]
            inv = [mixed(lambda r: inv[t][r * size : (r + 1) * size], rest[t]) for t in n]
        right = []
        for t, (c, h) in enumerate(items):
            bk = (k[t].astype(F32) * b[t]).astype(BF) * entry[c]
            right.append(jnp.concatenate([bk, (v[t].astype(F32) * b[t]).astype(BF)], axis=1))
        wu = [dot(inv[t].astype(BF), right[t]) for t in n]
        weight = [wu[t][:, :HD].astype(BF) for t in n]
        inject = [jnp.concatenate([jnp.zeros((CH, HD), F32), wu[t][:, HD:]], axis=1) for t in n]
        left = [jnp.concatenate([q[t] * entry[c], attn[t]], axis=1) for t, (c, h) in enumerate(items)]
        kept = [k[t] * leave[c] for t, (c, h) in enumerate(items)]
        for t, (c, h) in enumerate(items):
            state = state_ref[h]
            short = state.astype(BF)
            delta = (inject[t] - dot(weight[t], short)).astype(BF)
            state_ref[h] = state * keep[c] + dot_tn(kept[t], delta)
            result = dot(left[t], jnp.concatenate([short, delta], axis=0))
            p_ref[rows[c], h * 2 * HD : (h + 1) * 2 * HD] = result.astype(BF)
        return carry

    lax.fori_loop(0, ROWS // CH // per, chunks, 0)
    for h in range(nh):
        m_ref[h] = state_ref[h].astype(BF)


def finish_kernel(nh, split, where, m0, m1, m2, m3, s_ref, p_hbm, x_hbm, gain_ref, out_refs, final_ref, maps_ref, p_ref, x_ref, sems):
    sources = (p_hbm, *x_hbm)
    targets = (p_ref, *(x_ref.at[:, at * x_hbm[0].shape[1] : (at + 1) * x_hbm[0].shape[1]] for at in range(len(x_hbm))))
    copies = [pltpu.make_async_copy(a, b, sems.at[at]) for at, (a, b) in enumerate(zip(sources, targets))]
    for copy in copies:
        copy.start()
    for s, ref in enumerate((m0, m1, m2, m3)):
        maps_ref[lax.rem(where[0] - s + SIDE, SIDE)] = ref[...]
    states = [s_ref[h] for h in range(nh)]
    firsts = list(states)
    for z in range(SIDE):
        for h in range(nh):
            firsts[h] = jnp.where(where[0] == z, states[h], firsts[h])
        if split and z == SIDE - 1:
            break
        for h in range(nh):
            high = states[h].astype(BF)
            low = (states[h] - high.astype(F32)).astype(BF)
            a = maps_ref[z, h, :, :HD]
            states[h] = dot(a, high) + dot(a, low) + maps_ref[z, h, :, HD:].astype(F32)
    if not split:
        for h in range(nh):
            final_ref[h] = states[h]
    entries = [first.astype(BF) for first in firsts]
    for copy in copies:
        copy.wait()

    def finish(rows, outs, out_rows):
        for h in range(nh):
            pa = p_ref[rows, h * 2 * HD : h * 2 * HD + HD]
            pb = p_ref[rows, h * 2 * HD + HD : (h + 1) * 2 * HD]
            o = dot(pa, entries[h]) + pb.astype(F32)
            o = o * lax.rsqrt(jnp.mean(o * o, axis=-1, keepdims=True) + 1e-05) * gain_ref[...]
            x = x_ref[rows, h * HD : (h + 1) * HD].astype(F32)
            at = h % (nh // len(outs)) * HD
            outs[h * len(outs) // nh][out_rows, at : at + HD] = (x + o).astype(BF)

    if split:
        for s in range(SIDE):
            rows = pl.ds(pl.multiple_of(lax.rem(where[1] + s, SIDE) * 256, 256), 256)
            finish(rows, out_refs[s : s + 1], slice(None))
    else:

        def block(i, carry):
            rows = pl.ds(pl.multiple_of(i * 256, 256), 256)
            finish(rows, out_refs, rows)
            return carry

        lax.fori_loop(0, ROWS // 256, block, 0)


def finish_first_kernel(nh, *refs):
    finish_kernel(nh, False, *refs[:7], (refs[7],), *refs[8:9], refs[9:11], *refs[11:])


def finish_last_kernel(nh, *refs):
    finish_kernel(nh, True, *refs[:7], refs[7:9], refs[9], refs[10:14], None, *refs[14:])


def pack_kernel(where, w_ref, wb_ref, *out_refs):
    for g, heads in enumerate(GROUPS):
        width = len(heads) * HD
        for s in range(SIDE):
            for part in range(3):
                at = part * D + lax.rem(where[1] + s, SIDE) * (OWN * HD) + heads[0] * HD
                columns = w_ref[:, pl.ds(pl.multiple_of(at, HD), width)]
                out_refs[g * SIDE + s][:, part * width : (part + 1) * width] = columns
    source = lax.broadcasted_iota(jnp.int32, (HEADS, HD), 0)
    target = lax.broadcasted_iota(jnp.int32, (HEADS, HD), 1)
    for s in range(SIDE):
        chosen = (source == target + lax.rem(where[1] + s, SIDE) * OWN) & (target < OWN)
        out_refs[s][:, 3 * len(GROUPS[0]) * HD :] = dot(wb_ref[...], jnp.where(chosen, 1.0, 0.0).astype(BF)).astype(BF)


def join_kernel(*refs):
    for s in range(SIDE):
        refs[-1][s * HD : (s + 1) * HD] = refs[s][...]


def place_kernel(where, *refs):
    for s in range(SIDE):
        at = lax.rem(where[1] - s + SIDE, SIDE) * (OWN * HD)
        refs[-1][:, pl.ds(pl.multiple_of(at, OWN * HD), OWN * HD)] = refs[s][...]


def struct(shape, dtype=BF):
    return jax.ShapeDtypeStruct(shape, dtype)


def shards(residual, w_qkv, w_beta, beta_bias, norm_gain, out_gain, state_in, doc_start):
    z, y = lax.axis_index("z"), lax.axis_index("y")
    here = jnp.stack([z, y]).astype(jnp.int32)

    width = 3 * len(GROUPS[0]) * HD
    widths = (width + HD, width)
    packs = [struct((HD, wide)) for wide in widths for _ in range(SIDE)]
    packed = call(pack_kernel, "pack", packs, [SM, VM, VM], (here, w_qkv[0], w_beta[0]))
    weights = []
    for g in range(len(GROUPS)):
        mine = packed[g * SIDE : g * SIDE + SIDE]
        if weights:
            mine = after(tuple(mine), *first[1:])
        got = [mine[0]] + [shift(mine[s], "y", s) for s in range(1, SIDE)]
        first = first if weights else got
        joined = call(join_kernel, "join", [struct((SIDE * HD, widths[g]))], [VM] * SIDE, tuple(got))[0]
        weights.append(halves_around(joined, "z", *(weights[-1][3:5] if weights else ())))
    flat = [piece for pieces in weights for piece in pieces]
    x = after(residual[0], *weights[0][1:3], *got[1:])
    pieces = halves_around(x, "y", *weights[1][1:3])
    states = lax.dynamic_slice_in_dim(state_in[0], y * OWN, OWN, axis=0)

    for tick in range(TICKS):
        where = jnp.stack([z, y, doc_start[tick, 0] * GROUP - z * ROWS]).astype(jnp.int32)
        outs = [struct((ROWS, OWN * 2 * HD)), struct((OWN, HD, 2 * HD))]
        scratch = [
            pltpu.VMEM((ROWS, D), BF),
            pltpu.VMEM((D, widths[0]), BF),
            pltpu.VMEM((D, widths[1]), BF),
            pltpu.VMEM((ROWS, D), BF),
            pltpu.VMEM((ROWS, HD), F32),
            pltpu.VMEM((len(GROUPS), ROWS, width), BF),
            pltpu.VMEM((OWN, HD, 2 * HD), F32),
            pltpu.VMEM((1 + len(LEVELS), CH, CH), F32),
            pltpu.SemaphoreType.DMA((len(pieces),)),
            pltpu.SemaphoreType.DMA((len(flat),)),
        ]
        if tick == 0:
            outs.append(struct((ROWS, OWN * HD)))
        p, m, *rest = call(
            functools.partial(layer_kernel, tick),
            "layer",
            outs,
            [SM, SM] + [HBM] * len(pieces) + [VM] + [HBM] * len(flat),
            (where, beta_bias, *pieces, norm_gain, *flat),
            scratch=scratch,
            flops=8 * ROWS * D * OWN * HD,
            vmem=60 << 20,
        )
        maps = [m] + [shift(m, "z", s) for s in range(1, SIDE)]
        finish_scratch = [
            pltpu.VMEM((SIDE, OWN, HD, 2 * HD), BF),
            pltpu.VMEM((ROWS, OWN * 2 * HD), BF),
            pltpu.VMEM((ROWS, OWN * HD), BF),
        ]
        if tick + 1 < TICKS:
            pieces = []
            *outs, states = call(
                functools.partial(finish_first_kernel, OWN),
                "finish",
                [struct((ROWS, OWN * HD // len(GROUPS)))] * len(GROUPS) + [struct((OWN, HD, HD), F32)],
                [SM] + [VM] * 5 + [HBM] * 2 + [VM],
                (where, *maps, states, p, rest[0], out_gain),
                scratch=finish_scratch + [pltpu.SemaphoreType.DMA((2,))],
                vmem=60 << 20,
            )
            sections = lax.axis_size("section")
            pieces.extend(around(shift(outs[0], "section", 1, sections), "y", True))
            pieces.extend(shift(piece, "section", 1, sections) for piece in around(outs[1], "y", False))
        else:
            outs = call(
                functools.partial(finish_last_kernel, OWN),
                "finish_last",
                [struct((256, OWN * HD))] * SIDE,
                [SM] + [VM] * 5 + [HBM] * 3 + [VM],
                (where, *maps, states, p, pieces[0], pieces[SIDE], out_gain),
                scratch=finish_scratch + [pltpu.SemaphoreType.DMA((3,))],
                vmem=60 << 20,
            )
    outs = [outs[0]] + [shift(outs[s], "y", s) for s in range(1, SIDE)]
    out = call(place_kernel, "place", [struct((256, D))], [SM] + [VM] * SIDE, (here, *outs))[0]
    return out[None]


def solution(mesh):
    split = Mesh(mesh.devices.reshape(mesh.devices.shape[0], SIDE, SIDE), ("section", "z", "y"))
    wide = P("section", ("z", "y"), None)
    return jax.shard_map(
        shards,
        mesh=split,
        in_specs=(
            wide,
            wide,
            wide,
            P("section", None),
            P("section", None),
            P("section", None),
            P("section", None, None, None),
            P(None, "section"),
        ),
        out_specs=wide,
        check_vma=False,
    )
```
